512 devices in a mesh: row: 32 (over y_lo, x, core), col: 16 (over z, y_hi).
Axes of the slice: x: 4, y: 8 (y_hi: 2, y_lo: 4; y = y_hi * 4 + y_lo), z: 8, core: 2. Of those that a mesh axis runs over, the one named last changes fastest.
Arguments:
- vorticity_coefficients: bfloat16 [3, 512, 512, 512], P(None, 'row', 'col'), may hold values from -6 to 6
Outputs:
- enstrophy: float32 [512, 512, 512], P('row', 'col')
- normals: bfloat16 [3, 512, 512, 512], P(None, 'row', 'col')
The draws below stay inside these ranges and needn't reach their ends.
All inputs are finite; a program needn't handle non-finite values.
Results may differ from the reference program's by a relative error of at most 0.001.
Values sent between devices are 32-bit elements; how exact they have to be, the bound alone decides.
A program may use at most 64 MiB of HBM per device.

```python
import math
import jax
import jax.numpy as jnp
from jax import lax

N = 512


def levels(rng, dims, cuts, smallest, largest):
    def one(dim, shards_of):
        heights = jax.random.uniform(jax.random.fold_in(jax.random.fold_in(rng, 6), dim), (shards_of,), jnp.float32, smallest / len(cuts), largest / len(cuts))
        return jnp.repeat(jnp.exp(heights), dims[dim] // shards_of).reshape((-1,) + (1,) * (len(dims) - dim - 1))

    factor_of = one(*cuts[0])
    for cut in cuts[1:]:
        factor_of = factor_of * one(*cut)
    return factor_of


def centred(key, extent, width, limit, shards=(), held_as=jnp.bfloat16):
    gain = levels(key, extent, shards, -0.22, 0.18) if shards else 1.0
    array = jax.random.normal(key, extent, jnp.float32) * width * gain
    return jnp.minimum(jnp.maximum(array, -limit), limit).astype(held_as)


def setup_inputs(seed: int = 0) -> dict:
    arg_keys = jax.random.split(jax.random.key(seed), 2)
    vorticity_coefficients = centred(arg_keys[0], (3, N, N, N), 1.0, 6.0, ((1, 32), (2, 16)))
    return dict(vorticity_coefficients=vorticity_coefficients)


EXACT_MULTIPLY = lax.Precision.HIGHEST

def fourier_table(length):
    wave_number = jnp.arange(length, dtype=jnp.int32)[:, None]
    position = jnp.arange(length, dtype=jnp.int32)[None, :]
    nyquist = length // 2
    frequency = jnp.where(wave_number <= nyquist, wave_number, wave_number - nyquist)
    phase_index = (frequency * position % length).astype(jnp.int32)
    angle_value = phase_index.astype(jnp.float32) * (2.0 * math.pi / length)
    edge_mode = (wave_number == 0) | (wave_number == nyquist)
    hermitian_weight = jnp.where(edge_mode, math.sqrt(1.0 / length), math.sqrt(2.0 / length)).astype(jnp.float32)
    return jnp.where(wave_number <= nyquist, jnp.cos(angle_value), jnp.sin(angle_value)) * hermitian_weight

def reference(vorticity_coefficients):
    twiddle_table = fourier_table(N)

    def add_component(running, component):
        widened_input = component.astype(jnp.float32)
        first_axis_transform = jnp.einsum('uma,av->vum', widened_input, twiddle_table, precision=EXACT_MULTIPLY)
        along_second = jnp.einsum('xbq,by->xyq', first_axis_transform, twiddle_table, precision=EXACT_MULTIPLY)
        vort_field = jnp.einsum('xyq,qz->xyz', along_second, twiddle_table, precision=EXACT_MULTIPLY)
        return (running + 0.5 * vort_field * vort_field, None)
    enstrophy, unused = lax.scan(add_component, jnp.zeros((N, N, N), jnp.float32), vorticity_coefficients)
    step_x = 0.5 * (jnp.roll(enstrophy, -1, axis=0) - jnp.roll(enstrophy, 1, axis=0))
    step_y = 0.5 * (jnp.roll(enstrophy, -1, axis=1) - jnp.roll(enstrophy, 1, axis=1))
    step_z = 0.5 * (jnp.roll(enstrophy, -1, axis=2) - jnp.roll(enstrophy, 1, axis=2))
    magnitude = jnp.sqrt(step_x * step_x + step_y * step_y + step_z * step_z)
    inverse = 1.0 / jnp.maximum(magnitude, 1.0)
    normals = jnp.stack([-step_x * inverse, -step_y * inverse, -step_z * inverse], axis=0).astype(jnp.bfloat16)
    return (enstrophy, normals)
```

```python
import functools

import jax
import jax.numpy as jnp
import numpy as np
from jax import lax
from jax.experimental import pallas as pl
from jax.experimental.pallas import tpu as pltpu
from jax.sharding import PartitionSpec as P

MESH = pl.DeviceIdType.MESH
NT = (((1,), (1,)), ((), ()))
ORDER = (4, 3, 5, 2, 6, 1, 7)


def fourier_table(n):
    k = np.arange(n)[:, None]
    x = np.arange(n)[None, :]
    h = n // 2
    f = np.where(k <= h, k, k - h)
    angle = (f * x % n) * (2.0 * np.pi / n)
    weight = np.where((k == 0) | (k == h), np.sqrt(1.0 / n), np.sqrt(2.0 / n))
    return (np.where(k <= h, np.cos(angle), np.sin(angle)) * weight).astype(np.float32)


def split(table):
    high = table.astype(jnp.bfloat16)
    low = (table - high.astype(np.float32)).astype(jnp.bfloat16)
    return high, low


def tables(n):
    t = fourier_table(n)
    p, xc, i = np.meshgrid(np.arange(8), np.arange(8), np.arange(8), indexing="ij")
    x_order = (((p % 4) * 8 + xc) * 16 + (p // 4) * 8 + i).reshape(-1)
    bi, g = np.meshgrid(np.arange(16), np.arange(32), indexing="ij")
    b_order = (g * 16 + bi).reshape(-1)
    yh, zs, qj = np.meshgrid(np.arange(2), np.arange(8), np.arange(32), indexing="ij")
    q_order = ((zs * 2 + yh) * 32 + qj).reshape(-1)
    first = split(np.ascontiguousarray(t[:, x_order].T))
    second = split(np.ascontiguousarray(t[b_order].T))
    third = split(np.ascontiguousarray(t[q_order]))
    return first + second + third


def swap_groups(parts):
    lane = lax.broadcasted_iota(jnp.int32, parts[0].shape, 1)
    low_half = lane < 64
    even = (lane // 32) % 2 == 0
    p0, p1, p2, p3 = parts
    a0 = jnp.where(low_half, p0, pltpu.roll(p2, 64, 1))
    a2 = jnp.where(low_half, pltpu.roll(p0, 64, 1), p2)
    a1 = jnp.where(low_half, p1, pltpu.roll(p3, 64, 1))
    a3 = jnp.where(low_half, pltpu.roll(p1, 64, 1), p3)
    out = []
    for u, v in ((a0, a1), (a2, a3)):
        out.append(jnp.where(even, u, pltpu.roll(v, 32, 1)))
        out.append(jnp.where(even, pltpu.roll(u, 96, 1), v))
    return out


def kernel(
    x_ref, t1h, t1l, t2h, t2l, t3h, t3l, e_ref, n_ref,
    out1, r1, a, bh, bl, out2, cc, ch, cl, acc, ext, edge, halo,
    send, y_sem, x_sem, z_sem, e_sem, h_sem,
):
    row = lax.axis_index("row")
    col = lax.axis_index("col")
    y_lo, xc = row // 8, row % 8
    z, y_hi = col // 2, col % 2
    y = y_hi * 4 + y_lo

    def at_y(d):
        t = (y + d) % 8
        return t, {"row": (t % 4) * 8 + xc, "col": z * 2 + t // 4}

    def at_x(d):
        t = (xc + d) % 8
        return t, {"row": y_lo * 8 + t, "col": col}

    def at_z(d):
        t = (z + d) % 8
        return t, {"row": row, "col": t * 2 + y_hi}

    partner = at_y(4)[1]
    up = {"row": (row + 1) % 32, "col": col}
    down = {"row": (row + 31) % 32, "col": col}
    right = {"row": row, "col": (col + 1) % 16}
    left = {"row": row, "col": (col + 15) % 16}

    barrier = pltpu.get_barrier_semaphore()
    for d in ORDER:
        for at in (at_y, at_x, at_z):
            pl.semaphore_signal(barrier, inc=1, device_id=at(d)[1], device_id_type=MESH)
    for who in (up, down, right, left):
        pl.semaphore_signal(barrier, inc=1, device_id=who, device_id_type=MESH)

    def first(c):
        for n in range(2):
            data = x_ref[c, n * 256 : (n + 1) * 256, :]
            for m in range(2):
                rows = slice(m * 256, (m + 1) * 256)
                got = lax.dot_general(t1h[rows, :], data, NT, preferred_element_type=jnp.float32)
                got += lax.dot_general(t1l[rows, :], data, NT, preferred_element_type=jnp.float32)
                for h in range(2):
                    out1[c, n * 2 + h, m * 4 : (m + 1) * 4] = got[:, h * 128 : (h + 1) * 128].reshape(4, 64, 128)

    def remote(src, dst, s, r, who):
        pltpu.make_async_remote_copy(
            src_ref=src, dst_ref=dst, send_sem=s, recv_sem=r, device_id=who, device_id_type=MESH
        ).start()

    def send_y(c):
        for d in ORDER:
            t, who = at_y(d)
            remote(out1.at[c, :, t], r1.at[c, :, y], send.at[0], y_sem.at[c], who)
        r1[c, :, y] = out1[c, :, y]

    def wait(ref, sem):
        pltpu.make_async_copy(ref, ref, sem).wait()

    first(0)
    pl.semaphore_wait(barrier, 25)
    send_y(0)
    first(1)
    send_y(1)
    first(2)
    send_y(2)

    def gather_x(c):
        wait(r1.at[c, :, pl.ds(0, 7)], y_sem.at[c])
        for d in ORDER:
            t, who = at_x(d)
            remote(
                r1.at[c, :, :, pl.ds(pl.multiple_of(t * 8, 8), 8), :],
                a.at[c, :, :, pl.ds(pl.multiple_of(xc * 8, 8), 8), :],
                send.at[1], x_sem.at[c], who,
            )
        own = pl.ds(pl.multiple_of(xc * 8, 8), 8)
        a[c, :, :, own, :] = r1[c, :, :, own, :]
        wait(a.at[c, :, pl.ds(0, 7)], x_sem.at[c])

    def second(c):
        def tile(t, carry):
            for half in range(2):
                for quad in range(2):
                    for pair in range(2):
                        parts = []
                        for i in range(4):
                            rows = pl.ds(quad * 4 + i, 8, stride=8)
                            s = half * 4 + pair * 2
                            parts.append(jnp.concatenate([a[c, t, s, rows, :], a[c, t, s + 1, rows, :]], axis=0))
                        lanes = slice((half * 2 + quad) * 128, (half * 2 + quad + 1) * 128)
                        for j, part in enumerate(swap_groups(parts)):
                            high = part.astype(jnp.bfloat16)
                            low = (part - high.astype(jnp.float32)).astype(jnp.bfloat16)
                            rows = pl.ds(pl.multiple_of(t * 128 + (j * 32 + pair * 16), 16), 16)
                            bh[rows, lanes] = high
                            bl[rows, lanes] = low
            return carry

        lax.fori_loop(0, 4, tile, 0)
        for m in range(2):
            rows = slice(m * 256, (m + 1) * 256)
            got = jnp.dot(t2h[rows, :], bh[...], preferred_element_type=jnp.float32)
            got += jnp.dot(t2l[rows, :], bh[...], preferred_element_type=jnp.float32)
            got += jnp.dot(t2h[rows, :], bl[...], preferred_element_type=jnp.float32)
            out2[c, m * 4 : (m + 1) * 4] = got.reshape(4, 64, 512)
        for d in ORDER:
            t, who = at_z(d)
            remote(out2.at[c, t], cc.at[c, z], send.at[2], z_sem.at[c], who)
        cc[c, z] = out2[c, z]

    def third(c, after):
        wait(cc.at[c, pl.ds(0, 7)], z_sem.at[c])
        for quad in range(2):
            for half in range(2):
                for zq in range(2):
                    lanes = slice((half * 2 + quad) * 128, (half * 2 + quad + 1) * 128)
                    into = slice((half * 2 + zq) * 128, (half * 2 + zq + 1) * 128)
                    parts = [cc[c, zq * 4 + k, :, lanes] for k in range(4)]
                    for i, part in enumerate(swap_groups(parts)):
                        high = part.astype(jnp.bfloat16)
                        rows = slice((quad * 4 + i) * 64, (quad * 4 + i + 1) * 64)
                        ch[rows, into] = high
                        cl[rows, into] = (part - high.astype(jnp.float32)).astype(jnp.bfloat16)
            rows = slice(quad * 256, (quad + 1) * 256)
            got = jnp.dot(ch[rows, :], t3h[...], preferred_element_type=jnp.float32)
            got += jnp.dot(cl[rows, :], t3h[...], preferred_element_type=jnp.float32)
            got += jnp.dot(ch[rows, :], t3l[...], preferred_element_type=jnp.float32)
            level = (0.5 * got * got).reshape(4, 64, 512)
            planes = slice(quad * 4, (quad + 1) * 4)
            acc[planes] = jnp.where(c == 0, level, acc[planes] + level)
            after(quad)

    def step(c, carry):
        gather_x(c)
        second(c)

        @pl.when(c > 0)
        def _():
            third(c - 1, lambda quad: None)

        return carry

    lax.fori_loop(0, 3, step, 0)

    mine = pl.ds(pl.multiple_of(y_hi * 32, 32), 32)
    theirs = pl.ds(pl.multiple_of((1 - y_hi) * 32, 32), 32)

    def exchange(quad):
        planes = pl.ds(quad * 4, 4)
        slot = pl.ds(1 + y_hi * 8 + quad * 4, 4)
        remote(acc.at[planes, theirs, :], ext.at[slot], send.at[3], e_sem.at[0], partner)
        ext[slot] = acc[planes, mine, :]

    third(2, exchange)
    wait(acc.at[:, pl.ds(0, 32), :], e_sem.at[0])

    remote(ext.at[16], ext.at[0], send.at[4], h_sem.at[0], up)
    remote(ext.at[1], ext.at[17], send.at[5], h_sem.at[1], down)
    edge[0] = ext[1:17, 31, :]
    edge[1] = ext[1:17, 0, :]
    remote(edge.at[0], halo.at[0], send.at[6], h_sem.at[2], right)
    remote(edge.at[1], halo.at[1], send.at[7], h_sem.at[3], left)
    e_ref[...] = ext[1:17]
    wait(ext.at[0], h_sem.at[0])
    wait(ext.at[17], h_sem.at[1])
    wait(halo.at[0], h_sem.at[2])
    wait(halo.at[1], h_sem.at[3])

    place = lax.broadcasted_iota(jnp.int32, (32, 512), 0)

    def plane(i, carry):
        centre = ext[i + 1]
        step_x = 0.5 * (ext[i + 2] - ext[i])
        after = jnp.where(place == 31, halo[1, pl.ds(i, 1), :], pltpu.roll(centre, 31, 0))
        before = jnp.where(place == 0, halo[0, pl.ds(i, 1), :], pltpu.roll(centre, 1, 0))
        step_y = 0.5 * (after - before)
        step_z = 0.5 * (pltpu.roll(centre, 511, 1) - pltpu.roll(centre, 1, 1))
        square = step_x * step_x + step_y * step_y + step_z * step_z
        scale = -lax.rsqrt(jnp.maximum(square, 1.0))
        n_ref[0, i] = (step_x * scale).astype(jnp.bfloat16)
        n_ref[1, i] = (step_y * scale).astype(jnp.bfloat16)
        n_ref[2, i] = (step_z * scale).astype(jnp.bfloat16)
        return carry

    lax.fori_loop(0, 16, plane, 0)

    wait(out1.at[:, :, pl.ds(0, 7)], send.at[0])
    wait(a.at[:, :, pl.ds(0, 7)], send.at[1])
    wait(out2.at[:, pl.ds(0, 7)], send.at[2])
    wait(acc.at[:, pl.ds(0, 32), :], send.at[3])
    wait(ext.at[16], send.at[4])
    wait(ext.at[1], send.at[5])
    wait(edge.at[0], send.at[6])
    wait(edge.at[1], send.at[7])


def body(coefficients):
    members, span_b, span_q, length = coefficients.shape
    data = coefficients.reshape(members, span_b * span_q, length)
    whole = pl.BlockSpec(memory_space=pltpu.VMEM)
    f32, bf16 = jnp.float32, jnp.bfloat16
    return pl.pallas_call(
        kernel,
        out_shape=(
            jax.ShapeDtypeStruct((16, 32, 512), f32),
            jax.ShapeDtypeStruct((3, 16, 32, 512), bf16),
        ),
        in_specs=[whole] * 7,
        out_specs=(whole, whole),
        scratch_shapes=[
            pltpu.VMEM((3, 4, 8, 64, 128), f32),
            pltpu.VMEM((3, 4, 8, 64, 128), f32),
            pltpu.VMEM((3, 4, 8, 64, 128), f32),
            pltpu.VMEM((512, 512), bf16),
            pltpu.VMEM((512, 512), bf16),
            pltpu.VMEM((3, 8, 64, 512), f32),
            pltpu.VMEM((3, 8, 64, 512), f32),
            pltpu.VMEM((512, 512), bf16),
            pltpu.VMEM((512, 512), bf16),
            pltpu.VMEM((8, 64, 512), f32),
            pltpu.VMEM((18, 32, 512), f32),
            pltpu.VMEM((2, 16, 512), f32),
            pltpu.VMEM((2, 16, 512), f32),
            pltpu.SemaphoreType.DMA((8,)),
            pltpu.SemaphoreType.DMA((3,)),
            pltpu.SemaphoreType.DMA((3,)),
            pltpu.SemaphoreType.DMA((3,)),
            pltpu.SemaphoreType.DMA((1,)),
            pltpu.SemaphoreType.DMA((4,)),
        ],
        compiler_params=pltpu.CompilerParams(
            collective_id=0, has_side_effects=True, vmem_limit_bytes=56 * 1024 * 1024
        ),
        name="vorticity_normals",
    )(data, *tables(length))


def solution(mesh):
    return jax.shard_map(
        body,
        mesh=mesh,
        in_specs=(P(None, "row", "col", None),),
        out_specs=(P("row", "col", None), P(None, "row", "col", None)),
        check_vma=False,
    )
```

```python
import functools

import jax
import jax.numpy as jnp
import numpy as np
from jax import lax
from jax.experimental import pallas as pl
from jax.experimental.pallas import tpu as pltpu
from jax.sharding import PartitionSpec as P

MESH = pl.DeviceIdType.MESH
NT = (((1,), (1,)), ((), ()))
VMEM_MIB = 40
ORDER = (4, 3, 5, 2, 6, 1, 7)


def fourier_table(n):
    k = np.arange(n)[:, None]
    x = np.arange(n)[None, :]
    h = n // 2
    f = np.where(k <= h, k, k - h)
    angle = (f * x % n) * (2.0 * np.pi / n)
    weight = np.where((k == 0) | (k == h), np.sqrt(1.0 / n), np.sqrt(2.0 / n))
    return (np.where(k <= h, np.cos(angle), np.sin(angle)) * weight).astype(np.float32)


def split(table):
    high = table.astype(jnp.bfloat16)
    low = (table - high.astype(np.float32)).astype(jnp.bfloat16)
    return high, low


def tables(n):
    t = fourier_table(n)
    p, xc, i = np.meshgrid(np.arange(8), np.arange(8), np.arange(8), indexing="ij")
    x_order = (((p % 4) * 8 + xc) * 16 + (p // 4) * 8 + i).reshape(-1)
    h, zs, j = np.meshgrid(np.arange(2), np.arange(8), np.arange(32), indexing="ij")
    y_order = (zs * 64 + h * 32 + j).reshape(-1)
    bi, g = np.meshgrid(np.arange(16), np.arange(32), indexing="ij")
    b_order = (g * 16 + bi).reshape(-1)
    yh, zs, qj = np.meshgrid(np.arange(2), np.arange(8), np.arange(32), indexing="ij")
    q_order = ((zs * 2 + yh) * 32 + qj).reshape(-1)
    first = split(np.ascontiguousarray(t[:, x_order].T))
    second = split(np.ascontiguousarray(t[b_order][:, y_order].T))
    third = split(np.ascontiguousarray(t[q_order]))
    return np.stack(first + second + third)


def swap_groups(parts):
    lane = lax.broadcasted_iota(jnp.int32, parts[0].shape, 1)
    low_half = lane < 64
    even = (lane // 32) % 2 == 0
    p0, p1, p2, p3 = parts
    a0 = jnp.where(low_half, p0, pltpu.roll(p2, 64, 1))
    a2 = jnp.where(low_half, pltpu.roll(p0, 64, 1), p2)
    a1 = jnp.where(low_half, p1, pltpu.roll(p3, 64, 1))
    a3 = jnp.where(low_half, pltpu.roll(p1, 64, 1), p3)
    out = []
    for u, v in ((a0, a1), (a2, a3)):
        out.append(jnp.where(even, u, pltpu.roll(v, 32, 1)))
        out.append(jnp.where(even, pltpu.roll(u, 96, 1), v))
    return out


def kernel(
    x_hbm, t_hbm, e_ref, n_ref,
    x_ref, tab, out1, r1, a, bh, bl, out2, cc, ch, cl, acc, ext, edge, halo, nrm,
    load, store, send, y_sem, x_sem, z_sem, e_sem, h_sem,
):
    row = lax.axis_index("row")
    col = lax.axis_index("col")
    y_lo, xc = row // 8, row % 8
    z, u = col // 2, col % 2
    y = u * 4 + y_lo

    def at_y(d):
        t = (y + d) % 8
        return t, {"row": (t % 4) * 8 + xc, "col": z * 2 + t // 4}

    def at_x(d):
        t = (xc + d) % 8
        return t, {"row": y_lo * 8 + t, "col": col}

    def at_z(d):
        t = (z + d) % 8
        return t, {"row": row, "col": t * 2 + u}

    partner = at_y(4)[1]
    up = {"row": (row + 1) % 32, "col": col}
    down = {"row": (row + 31) % 32, "col": col}
    beside = {"row": row, "col": (col + 15 + 2 * u) % 16}
    beyond = {"row": row, "col": (col + 2 + 12 * u) % 16}

    barrier = pltpu.get_barrier_semaphore()
    for d in ORDER:
        for at in (at_y, at_x, at_z):
            pl.semaphore_signal(barrier, inc=1, device_id=at(d)[1], device_id_type=MESH)
    for who in (up, down, beside):
        pl.semaphore_signal(barrier, inc=1, device_id=who, device_id_type=MESH)

    def wait(ref, sem):
        pltpu.make_async_copy(ref, ref, sem).wait()

    loads = [pltpu.make_async_copy(t_hbm.at[pl.ds(2 * i, 2)], tab.at[pl.ds(2 * i, 2)], load.at[i]) for i in range(3)]
    loads += [pltpu.make_async_copy(x_hbm.at[c], x_ref.at[c], load.at[3 + c]) for c in range(3)]
    for i in (0, 3, 4, 5, 1, 2):
        loads[i].start()

    def remote(src, dst, s, r, who):
        pltpu.make_async_remote_copy(
            src_ref=src, dst_ref=dst, send_sem=s, recv_sem=r, device_id=who, device_id_type=MESH
        ).start()

    def first(c, n):
        data = x_ref[c, n * 256 : (n + 1) * 256, :]
        for m in range(2):
            rows = slice(m * 256, (m + 1) * 256)
            got = lax.dot_general(tab[0, rows, :], data, NT, preferred_element_type=jnp.float32)
            got += lax.dot_general(tab[1, rows, :], data, NT, preferred_element_type=jnp.float32)
            for h in range(2):
                out1[c, n * 2 + h, m * 4 : (m + 1) * 4] = got[:, h * 128 : (h + 1) * 128].reshape(4, 64, 128)

    def send_y(c, n):
        two = pl.ds(n * 2, 2)
        for d in ORDER:
            t, who = at_y(d)
            remote(out1.at[c, two, t], r1.at[c, two, y], send.at[0], y_sem.at[c * 2 + n], who)
        r1[c, two, y] = out1[c, two, y]

    loads[0].wait()
    for c in range(3):
        loads[3 + c].wait()
        for n in range(2):
            first(c, n)
            if c == 0 and n == 0:
                pl.semaphore_wait(barrier, 24)
            send_y(c, n)
    loads[1].wait()
    loads[2].wait()

    def gather_x(c, n):
        two = pl.ds(n * 2, 2)
        own = pl.ds(pl.multiple_of(xc * 8, 8), 8)
        wait(r1.at[c, two, pl.ds(0, 7)], y_sem.at[c * 2 + n])
        for d in ORDER:
            t, who = at_x(d)
            remote(
                r1.at[c, two, :, pl.ds(pl.multiple_of(t * 8, 8), 8), :],
                a.at[c, two, :, own, :],
                send.at[1], x_sem.at[c * 2 + n], who,
            )
        a[c, two, :, own, :] = r1[c, two, :, own, :]
        wait(a.at[c, two, pl.ds(0, 7)], x_sem.at[c * 2 + n])

    def second(c, n):
        def tile(t, carry):
            for half in range(2):
                for quad in range(2):
                    for pair in range(2):
                        parts = []
                        for i in range(4):
                            rows = pl.ds(quad * 4 + i, 8, stride=8)
                            s = half * 4 + pair * 2
                            parts.append(jnp.concatenate([a[c, t, s, rows, :], a[c, t, s + 1, rows, :]], axis=0))
                        lanes = slice((half * 2 + quad) * 128, (half * 2 + quad + 1) * 128)
                        for j, part in enumerate(swap_groups(parts)):
                            high = part.astype(jnp.bfloat16)
                            low = (part - high.astype(jnp.float32)).astype(jnp.bfloat16)
                            rows = pl.ds(pl.multiple_of(t * 128 + (j * 32 + pair * 16), 16), 16)
                            bh[rows, lanes] = high
                            bl[rows, lanes] = low
            return carry

        lax.fori_loop(2 * n, 2 * n + 2, tile, 0)
        depth = slice(n * 256, (n + 1) * 256)
        for o in range(2):
            rows = pl.ds(pl.multiple_of((u if o else 1 - u) * 256, 256), 256)
            got = jnp.dot(tab[2, rows, depth], bh[depth, :], preferred_element_type=jnp.float32)
            got += jnp.dot(tab[3, rows, depth], bh[depth, :], preferred_element_type=jnp.float32)
            got += jnp.dot(tab[2, rows, depth], bl[depth, :], preferred_element_type=jnp.float32)
            got = got.reshape(8, 32, 512)
            if n == 0:
                out2[c, o] = got
            else:
                out2[c, o] += got
                for d in ORDER:
                    t, who = at_z(d)
                    remote(out2.at[c, o, t], cc.at[c, o, z], send.at[2], z_sem.at[c * 2 + o], who)
                cc[c, o, z] = out2[c, o, z]

    def third(c, o):
        wait(cc.at[c, o, pl.ds(0, 7)], z_sem.at[c * 2 + o])
        for quad in range(2):
            for half in range(2):
                for zq in range(2):
                    lanes = slice((half * 2 + quad) * 128, (half * 2 + quad + 1) * 128)
                    into = slice((half * 2 + zq) * 128, (half * 2 + zq + 1) * 128)
                    parts = [cc[c, o, zq * 4 + k, :, lanes] for k in range(4)]
                    for i, part in enumerate(swap_groups(parts)):
                        high = part.astype(jnp.bfloat16)
                        rows = slice((quad * 4 + i) * 32, (quad * 4 + i + 1) * 32)
                        ch[rows, into] = high
                        cl[rows, into] = (part - high.astype(jnp.float32)).astype(jnp.bfloat16)
        got = jnp.dot(ch[...], tab[4], preferred_element_type=jnp.float32)
        got += jnp.dot(cl[...], tab[4], preferred_element_type=jnp.float32)
        got += jnp.dot(ch[...], tab[5], preferred_element_type=jnp.float32)
        return (0.5 * got * got).reshape(8, 32, 512)

    def step(c, carry):
        for n in range(2):
            gather_x(c, n)
            second(c, n)

        @pl.when(c > 0)
        def _():
            def half(o, carry):
                level = third(c - 1, o)
                acc[o] = jnp.where(c == 1, level, acc[o] + level)
                return carry

            lax.fori_loop(0, 2, half, 0)

        return carry

    lax.fori_loop(0, 3, step, 0)

    slot = pl.ds(1 + u * 8, 8)
    other = pl.ds(1 + (1 - u) * 8, 8)

    acc[0] += third(2, 0)
    remote(acc.at[0], ext.at[slot], send.at[3], e_sem.at[0], partner)
    top, bottom = acc[0, :, 0, :], acc[0, :, 31, :]
    edge[2] = jnp.where(u == 0, bottom, top)
    remote(edge.at[2], halo.at[u, u], send.at[4], h_sem.at[4], beyond)
    halo[1 - u, u] = jnp.where(u == 0, top, bottom)

    acc[1] += third(2, 1)
    top, bottom = acc[1, :, 0, :], acc[1, :, 31, :]
    edge[0] = jnp.where(u == 0, bottom, top)
    edge[1] = jnp.where(u == 0, top, bottom)
    remote(edge.at[0], halo.at[u, u], send.at[5], h_sem.at[2], partner)
    remote(edge.at[1], halo.at[1 - u, u], send.at[6], h_sem.at[3], beside)
    ext[slot] = acc[1]

    place = lax.broadcasted_iota(jnp.int32, (32, 512), 0)

    def plane(i, carry):
        centre = ext[i + 1]
        step_x = 0.5 * (ext[i + 2] - ext[i])
        after = jnp.where(place == 31, halo[1, i // 8, pl.ds(i % 8, 1), :], pltpu.roll(centre, 31, 0))
        before = jnp.where(place == 0, halo[0, i // 8, pl.ds(i % 8, 1), :], pltpu.roll(centre, 1, 0))
        step_y = 0.5 * (after - before)
        step_z = 0.5 * (pltpu.roll(centre, 511, 1) - pltpu.roll(centre, 1, 1))
        square = step_x * step_x + step_y * step_y + step_z * step_z
        scale = -lax.rsqrt(jnp.maximum(square, 1.0))
        nrm[0, i] = (step_x * scale).astype(jnp.bfloat16)
        nrm[1, i] = (step_y * scale).astype(jnp.bfloat16)
        nrm[2, i] = (step_z * scale).astype(jnp.bfloat16)
        return carry

    wait(halo.at[0, 0], h_sem.at[4])
    lax.fori_loop(1 + 8 * u, 7 + 8 * u, plane, 0)

    wait(halo.at[0, 0], h_sem.at[2])
    wait(halo.at[0, 0], h_sem.at[3])
    wait(ext.at[pl.ds(1, 8)], e_sem.at[0])
    remote(ext.at[16], ext.at[0], send.at[7], h_sem.at[0], up)
    remote(ext.at[1], ext.at[17], send.at[8], h_sem.at[1], down)
    level_out = pltpu.make_async_copy(ext.at[pl.ds(1, 16)], e_ref, store.at[0])
    level_out.start()
    lax.fori_loop(7 - 6 * u, 15 - 6 * u, plane, 0)
    inner = pl.ds(1, 14)
    inner_out = pltpu.make_async_copy(nrm.at[:, inner], n_ref.at[:, inner], store.at[1])
    inner_out.start()
    wait(ext.at[0], h_sem.at[0])
    wait(ext.at[17], h_sem.at[1])
    outs = []
    for k, i in enumerate((0, 15)):
        plane(i, 0)
        outs.append(pltpu.make_async_copy(nrm.at[:, i], n_ref.at[:, i], store.at[2 + k]))
        outs[-1].start()

    wait(out1.at[:, :, pl.ds(0, 7)], send.at[0])
    wait(a.at[:, :, pl.ds(0, 7)], send.at[1])
    wait(out2.at[:, :, pl.ds(0, 7)], send.at[2])
    wait(acc.at[0], send.at[3])
    wait(edge.at[0], send.at[4])
    wait(edge.at[0], send.at[5])
    wait(edge.at[0], send.at[6])
    wait(ext.at[16], send.at[7])
    wait(ext.at[1], send.at[8])
    level_out.wait()
    inner_out.wait()
    for out in outs:
        out.wait()


def body(coefficients):
    members, span_b, span_q, length = coefficients.shape
    data = coefficients.reshape(members, span_b * span_q, length)
    apart = pl.BlockSpec(memory_space=pl.ANY)
    f32, bf16 = jnp.float32, jnp.bfloat16
    return pl.pallas_call(
        kernel,
        out_shape=(
            jax.ShapeDtypeStruct((16, 32, 512), f32),
            jax.ShapeDtypeStruct((3, 16, 32, 512), bf16),
        ),
        in_specs=[pl.BlockSpec(memory_space=pltpu.HBM)] * 2,
        out_specs=(apart, apart),
        scratch_shapes=[
            pltpu.VMEM((3, 512, 512), bf16),
            pltpu.VMEM((6, 512, 512), bf16),
            pltpu.VMEM((3, 4, 8, 64, 128), f32),
            pltpu.VMEM((3, 4, 8, 64, 128), f32),
            pltpu.VMEM((3, 4, 8, 64, 128), f32),
            pltpu.VMEM((512, 512), bf16),
            pltpu.VMEM((512, 512), bf16),
            pltpu.VMEM((3, 2, 8, 32, 512), f32),
            pltpu.VMEM((3, 2, 8, 32, 512), f32),
            pltpu.VMEM((256, 512), bf16),
            pltpu.VMEM((256, 512), bf16),
            pltpu.VMEM((2, 8, 32, 512), f32),
            pltpu.VMEM((18, 32, 512), f32),
            pltpu.VMEM((3, 8, 512), f32),
            pltpu.VMEM((2, 2, 8, 512), f32),
            pltpu.VMEM((3, 16, 32, 512), bf16),
            pltpu.SemaphoreType.DMA((6,)),
            pltpu.SemaphoreType.DMA((4,)),
            pltpu.SemaphoreType.DMA((9,)),
            pltpu.SemaphoreType.DMA((6,)),
            pltpu.SemaphoreType.DMA((6,)),
            pltpu.SemaphoreType.DMA((6,)),
            pltpu.SemaphoreType.DMA((1,)),
            pltpu.SemaphoreType.DMA((5,)),
        ],
        compiler_params=pltpu.CompilerParams(
            collective_id=0, has_side_effects=True, vmem_limit_bytes=VMEM_MIB * 1024 * 1024
        ),
        name="vorticity_normals",
    )(data, tables(length))


def solution(mesh):
    return jax.shard_map(
        body,
        mesh=mesh,
        in_specs=(P(None, "row", "col", None),),
        out_specs=(P("row", "col", None), P(None, "row", "col", None)),
        check_vma=False,
    )
```

```python
import functools

import jax
import jax.numpy as jnp
import numpy as np
from jax import lax
from jax.experimental import pallas as pl
from jax.experimental.pallas import tpu as pltpu
from jax.sharding import PartitionSpec as P

MESH = pl.DeviceIdType.MESH
NT = (((1,), (1,)), ((), ()))
VMEM_MIB = 51
CHUNKS = ((0, 1, 6, 7), (2, 3, 4, 5))
ORDER = (4, 3, 5, 2, 6, 1, 7)


def fourier_table(n):
    k = np.arange(n)[:, None]
    x = np.arange(n)[None, :]
    h = n // 2
    f = np.where(k <= h, k, k - h)
    angle = (f * x % n) * (2.0 * np.pi / n)
    weight = np.where((k == 0) | (k == h), np.sqrt(1.0 / n), np.sqrt(2.0 / n))
    return (np.where(k <= h, np.cos(angle), np.sin(angle)) * weight).astype(np.float32)


def split(table):
    high = table.astype(jnp.bfloat16)
    low = (table - high.astype(np.float32)).astype(jnp.bfloat16)
    return high, low


def tables(n):
    t = fourier_table(n)
    planes = np.array(CHUNKS)
    k, p, xc, i = np.meshgrid(np.arange(2), np.arange(8), np.arange(8), np.arange(4), indexing="ij")
    x_order = (((p % 4) * 8 + xc) * 16 + (p // 4) * 8 + planes[k, i]).reshape(-1)
    h, zs, j = np.meshgrid(np.arange(2), np.arange(8), np.arange(32), indexing="ij")
    y_order = (zs * 64 + h * 32 + j).reshape(-1)
    bi, g = np.meshgrid(np.arange(16), np.arange(32), indexing="ij")
    b_order = (g * 16 + bi).reshape(-1)
    yh, zs, qj = np.meshgrid(np.arange(2), np.arange(8), np.arange(32), indexing="ij")
    q_order = ((zs * 2 + yh) * 32 + qj).reshape(-1)
    first = split(np.ascontiguousarray(t[:, x_order].T))
    second = split(np.ascontiguousarray(t[b_order][:, y_order].T))
    third = split(np.ascontiguousarray(t[q_order]))
    return np.stack(first + second + third)


def swap_groups(parts):
    lane = lax.broadcasted_iota(jnp.int32, parts[0].shape, 1)
    low_half = lane < 64
    even = (lane // 32) % 2 == 0
    p0, p1, p2, p3 = parts
    a0 = jnp.where(low_half, p0, pltpu.roll(p2, 64, 1))
    a2 = jnp.where(low_half, pltpu.roll(p0, 64, 1), p2)
    a1 = jnp.where(low_half, p1, pltpu.roll(p3, 64, 1))
    a3 = jnp.where(low_half, pltpu.roll(p1, 64, 1), p3)
    out = []
    for u, v in ((a0, a1), (a2, a3)):
        out.append(jnp.where(even, u, pltpu.roll(v, 32, 1)))
        out.append(jnp.where(even, pltpu.roll(u, 96, 1), v))
    return out


def kernel(
    x_hbm, t_hbm, e_ref, n_ref,
    x_ref, tab, out1, r1, a, bh, bl, out2, cc, ch, cl, acc, ext, edge, halo, nrm,
    load, store, send, y_sem, x_sem, z_sem, e_sem, h_sem,
):
    row = lax.axis_index("row")
    col = lax.axis_index("col")
    y_lo, xc = row // 8, row % 8
    z, u = col // 2, col % 2
    y = u * 4 + y_lo

    def at_y(d):
        t = (y + d) % 8
        return t, {"row": (t % 4) * 8 + xc, "col": z * 2 + t // 4}

    def at_x(d):
        t = (xc + d) % 8
        return t, {"row": y_lo * 8 + t, "col": col}

    def at_z(d):
        t = (z + d) % 8
        return t, {"row": row, "col": t * 2 + u}

    partner = at_y(4)[1]
    up = {"row": (row + 1) % 32, "col": col}
    down = {"row": (row + 31) % 32, "col": col}
    beside = {"row": row, "col": (col + 15 + 2 * u) % 16}
    beyond = {"row": row, "col": (col + 2 + 12 * u) % 16}

    barrier = pltpu.get_barrier_semaphore()
    for d in ORDER:
        for at in (at_y, at_x, at_z):
            pl.semaphore_signal(barrier, inc=1, device_id=at(d)[1], device_id_type=MESH)
    for who in (up, down, beside):
        pl.semaphore_signal(barrier, inc=1, device_id=who, device_id_type=MESH)

    def wait(ref, sem):
        pltpu.make_async_copy(ref, ref, sem).wait()

    loads = [pltpu.make_async_copy(t_hbm.at[pl.ds(2 * i, 2)], tab.at[pl.ds(2 * i, 2)], load.at[i]) for i in range(3)]
    loads += [pltpu.make_async_copy(x_hbm.at[c], x_ref.at[c], load.at[3 + c]) for c in range(3)]
    for i in (0, 3, 4, 5, 1, 2):
        loads[i].start()

    def remote(src, dst, s, r, who):
        pltpu.make_async_remote_copy(
            src_ref=src, dst_ref=dst, send_sem=s, recv_sem=r, device_id=who, device_id_type=MESH
        ).start()

    upper = lax.broadcasted_iota(jnp.int32, (32, 8, 256), 1) < 4

    def first(c, k):
        rows = slice(k * 256, (k + 1) * 256)
        got = []
        for w in range(2):
            data = x_ref[c, w * 256 : (w + 1) * 256, :]
            part = lax.dot_general(tab[0, rows, :], data, NT, preferred_element_type=jnp.float32)
            part += lax.dot_general(tab[1, rows, :], data, NT, preferred_element_type=jnp.float32)
            got.append(part.reshape(32, 8, 256))
        even = jnp.where(upper, got[0], pltpu.roll(got[1], 4, 1))
        odd = jnp.where(upper, pltpu.roll(got[0], 4, 1), got[1])
        both = jnp.stack([even, odd], axis=1)
        for t in range(2):
            out1[c, k, t] = both[:, :, :, t * 128 : (t + 1) * 128].reshape(8, 64, 128)

    def send_y(c, k):
        for d in ORDER:
            t, who = at_y(d)
            remote(out1.at[c, k, :, t], r1.at[c, k, :, y], send.at[0], y_sem.at[k * 3 + c], who)
        r1[c, k, :, y] = out1[c, k, :, y]

    loads[0].wait()
    for k in range(2):
        for c in range(3):
            if k == 0:
                loads[3 + c].wait()
            first(c, k)
            if c == 0 and k == 0:
                pl.semaphore_wait(barrier, 24)
            send_y(c, k)
    loads[1].wait()
    loads[2].wait()

    def gather_x(c, k):
        own = pl.ds(pl.multiple_of(xc * 8, 8), 8)
        wait(r1.at[c, k, :, pl.ds(0, 7)], y_sem.at[k * 3 + c])
        for d in ORDER:
            t, who = at_x(d)
            remote(
                r1.at[c, k, :, :, pl.ds(pl.multiple_of(t * 8, 8), 8), :],
                a.at[c, k, :, :, own, :],
                send.at[1], x_sem.at[k * 3 + c], who,
            )
        a[c, k, :, :, own, :] = r1[c, k, :, :, own, :]
        wait(a.at[c, k, :, pl.ds(0, 7)], x_sem.at[k * 3 + c])

    def second(c, k):
        def tile(t, carry):
            for w in range(2):
                for half in range(2):
                    for pair in range(2):
                        parts = []
                        for i in range(4):
                            rows = pl.ds(w * 4 + i, 8, stride=8)
                            s = half * 4 + pair * 2
                            parts.append(
                                jnp.concatenate([a[c, k, t, s, rows, :], a[c, k, t, s + 1, rows, :]], axis=0)
                            )
                        lanes = slice(half * 128, (half + 1) * 128)
                        for j, part in enumerate(swap_groups(parts)):
                            high = part.astype(jnp.bfloat16)
                            low = (part - high.astype(jnp.float32)).astype(jnp.bfloat16)
                            rows = pl.ds(pl.multiple_of(t * 128 + (w * 256 + j * 32 + pair * 16), 16), 16)
                            bh[rows, lanes] = high
                            bl[rows, lanes] = low
            return carry

        lax.fori_loop(0, 2, tile, 0)
        for o in range(2):
            rows = pl.ds(pl.multiple_of((u if o else 1 - u) * 256, 256), 256)
            got = jnp.dot(tab[2, rows, :], bh[...], preferred_element_type=jnp.float32)
            got += jnp.dot(tab[3, rows, :], bh[...], preferred_element_type=jnp.float32)
            got += jnp.dot(tab[2, rows, :], bl[...], preferred_element_type=jnp.float32)
            out2[c, k, o] = got.reshape(8, 32, 256)
            for d in ORDER:
                t, who = at_z(d)
                remote(
                    out2.at[c, k, o, t], cc.at[c, k, o, z],
                    send.at[2], z_sem.at[(k * 3 + c) * 2 + o], who,
                )
            cc[c, k, o, z] = out2[c, k, o, z]

    def third(c, k, o):
        wait(cc.at[c, k, o, pl.ds(0, 7)], z_sem.at[(k * 3 + c) * 2 + o])
        for half in range(2):
            for zq in range(2):
                lanes = slice(half * 128, (half + 1) * 128)
                into = slice((half * 2 + zq) * 128, (half * 2 + zq + 1) * 128)
                parts = [cc[c, k, o, zq * 4 + i, :, lanes] for i in range(4)]
                for i, part in enumerate(swap_groups(parts)):
                    high = part.astype(jnp.bfloat16)
                    rows = slice(i * 32, (i + 1) * 32)
                    ch[rows, into] = high
                    cl[rows, into] = (part - high.astype(jnp.float32)).astype(jnp.bfloat16)
        got = jnp.dot(ch[...], tab[4], preferred_element_type=jnp.float32)
        got += jnp.dot(cl[...], tab[4], preferred_element_type=jnp.float32)
        got += jnp.dot(ch[...], tab[5], preferred_element_type=jnp.float32)
        level = (0.5 * got * got).reshape(4, 32, 512)
        acc[k, o] = jnp.where(c == 0, level, acc[k, o] + level)

    base = 1 + u * 8

    def step(j, carry):
        @pl.when(j < 6)
        def _():
            gather_x(j % 3, j // 3)
            second(j % 3, j // 3)

        @pl.when(j > 1)
        def _():
            c, k = (j - 2) % 3, (j - 2) // 3

            def half(o, carry):
                third(c, k, o)

                @pl.when((c == 2) & (k == 0) & (o == 0))
                def _():
                    for i in (0, 2):
                        planes = pl.ds(base + 3 * i, 2)
                        remote(acc.at[0, 0, pl.ds(i, 2)], ext.at[planes], send.at[3], e_sem.at[0], partner)

                @pl.when((c == 2) & (k == 1) & (o == 0))
                def _():
                    remote(acc.at[1, 0], ext.at[pl.ds(base + 2, 4)], send.at[3], e_sem.at[1], partner)

                return carry

            lax.fori_loop(0, 2, half, 0)

        return carry

    lax.fori_loop(0, 8, step, 0)

    def line(o, r):
        first_four, last_four = acc[0, o, :, r, :], acc[1, o, :, r, :]
        return jnp.concatenate([first_four[:2], last_four, first_four[2:]], axis=0)

    top, bottom = line(0, 0), line(0, 31)
    edge[2] = jnp.where(u == 0, bottom, top)
    remote(edge.at[2], halo.at[u, u], send.at[4], h_sem.at[4], beyond)
    halo[1 - u, u] = jnp.where(u == 0, top, bottom)
    top, bottom = line(1, 0), line(1, 31)
    edge[0] = jnp.where(u == 0, bottom, top)
    edge[1] = jnp.where(u == 0, top, bottom)
    remote(edge.at[0], halo.at[u, u], send.at[5], h_sem.at[2], partner)
    remote(edge.at[1], halo.at[1 - u, u], send.at[6], h_sem.at[3], beside)
    for k in range(2):
        for i, at in enumerate(CHUNKS[k]):
            ext[base + at] = acc[k, 1, i]

    place = lax.broadcasted_iota(jnp.int32, (32, 512), 0)

    def plane(i, carry):
        centre = ext[i + 1]
        step_x = 0.5 * (ext[i + 2] - ext[i])
        after = jnp.where(place == 31, halo[1, i // 8, pl.ds(i % 8, 1), :], pltpu.roll(centre, 31, 0))
        before = jnp.where(place == 0, halo[0, i // 8, pl.ds(i % 8, 1), :], pltpu.roll(centre, 1, 0))
        step_y = 0.5 * (after - before)
        step_z = 0.5 * (pltpu.roll(centre, 511, 1) - pltpu.roll(centre, 1, 1))
        square = step_x * step_x + step_y * step_y + step_z * step_z
        scale = -lax.rsqrt(jnp.maximum(square, 1.0))
        nrm[0, i] = (step_x * scale).astype(jnp.bfloat16)
        nrm[1, i] = (step_y * scale).astype(jnp.bfloat16)
        nrm[2, i] = (step_z * scale).astype(jnp.bfloat16)
        return carry

    wait(ext.at[pl.ds(1, 4)], e_sem.at[0])
    remote(ext.at[16], ext.at[0], send.at[7], h_sem.at[0], up)
    remote(ext.at[1], ext.at[17], send.at[8], h_sem.at[1], down)
    mine, theirs = pl.ds(8 * u, 8), pl.ds(8 * (1 - u), 8)
    level_mine = pltpu.make_async_copy(ext.at[pl.ds(base, 8)], e_ref.at[mine], store.at[0])
    level_mine.start()
    wait(halo.at[0, 0], h_sem.at[4])
    lax.fori_loop(1 + 8 * u, 7 + 8 * u, plane, 0)
    wait(halo.at[0, 0], h_sem.at[2])
    wait(halo.at[0, 0], h_sem.at[3])
    lax.fori_loop(7, 9, plane, 0)
    wait(ext.at[0], h_sem.at[0])
    wait(ext.at[17], h_sem.at[1])
    plane(0, 0)
    plane(15, 0)
    normals_mine = pltpu.make_async_copy(nrm.at[:, mine], n_ref.at[:, mine], store.at[1])
    normals_mine.start()
    wait(ext.at[pl.ds(1, 4)], e_sem.at[1])
    level_theirs = pltpu.make_async_copy(ext.at[pl.ds(9 - 8 * u, 8)], e_ref.at[theirs], store.at[2])
    level_theirs.start()
    lax.fori_loop(9 - 8 * u, 15 - 8 * u, plane, 0)
    normals_theirs = pltpu.make_async_copy(nrm.at[:, theirs], n_ref.at[:, theirs], store.at[3])
    normals_theirs.start()

    wait(out1.at[:, :, :, pl.ds(0, 7)], send.at[0])
    wait(a.at[:, :, :, pl.ds(0, 7)], send.at[1])
    wait(out2.at[:, :, :, pl.ds(0, 7)], send.at[2])
    wait(acc.at[0], send.at[3])
    wait(edge.at[0], send.at[4])
    wait(edge.at[0], send.at[5])
    wait(edge.at[0], send.at[6])
    wait(ext.at[16], send.at[7])
    wait(ext.at[1], send.at[8])
    for out in (level_mine, normals_mine, level_theirs, normals_theirs):
        out.wait()


def body(coefficients):
    members, span_b, span_q, length = coefficients.shape
    data = coefficients.reshape(members, span_b * span_q, length)
    apart = pl.BlockSpec(memory_space=pl.ANY)
    f32, bf16 = jnp.float32, jnp.bfloat16
    return pl.pallas_call(
        kernel,
        out_shape=(
            jax.ShapeDtypeStruct((16, 32, 512), f32),
            jax.ShapeDtypeStruct((3, 16, 32, 512), bf16),
        ),
        in_specs=[pl.BlockSpec(memory_space=pltpu.HBM)] * 2,
        out_specs=(apart, apart),
        scratch_shapes=[
            pltpu.VMEM((3, 512, 512), bf16),
            pltpu.VMEM((6, 512, 512), bf16),
            pltpu.VMEM((3, 2, 2, 8, 64, 128), f32),
            pltpu.VMEM((3, 2, 2, 8, 64, 128), f32),
            pltpu.VMEM((3, 2, 2, 8, 64, 128), f32),
            pltpu.VMEM((512, 256), bf16),
            pltpu.VMEM((512, 256), bf16),
            pltpu.VMEM((3, 2, 2, 8, 32, 256), f32),
            pltpu.VMEM((3, 2, 2, 8, 32, 256), f32),
            pltpu.VMEM((128, 512), bf16),
            pltpu.VMEM((128, 512), bf16),
            pltpu.VMEM((2, 2, 4, 32, 512), f32),
            pltpu.VMEM((18, 32, 512), f32),
            pltpu.VMEM((3, 8, 512), f32),
            pltpu.VMEM((2, 2, 8, 512), f32),
            pltpu.VMEM((3, 16, 32, 512), bf16),
            pltpu.SemaphoreType.DMA((6,)),
            pltpu.SemaphoreType.DMA((4,)),
            pltpu.SemaphoreType.DMA((9,)),
            pltpu.SemaphoreType.DMA((6,)),
            pltpu.SemaphoreType.DMA((6,)),
            pltpu.SemaphoreType.DMA((12,)),
            pltpu.SemaphoreType.DMA((2,)),
            pltpu.SemaphoreType.DMA((5,)),
        ],
        compiler_params=pltpu.CompilerParams(
            collective_id=0, has_side_effects=True, vmem_limit_bytes=VMEM_MIB * 1024 * 1024
        ),
        name="vorticity_normals",
    )(data, tables(length))


def solution(mesh):
    return jax.shard_map(
        body,
        mesh=mesh,
        in_specs=(P(None, "row", "col", None),),
        out_specs=(P("row", "col", None), P(None, "row", "col", None)),
        check_vma=False,
    )
```

```python
import functools

import jax
import jax.numpy as jnp
import numpy as np
from jax import lax
from jax.experimental import pallas as pl
from jax.experimental.pallas import tpu as pltpu
from jax.sharding import PartitionSpec as P

MESH = pl.DeviceIdType.MESH
NT = (((1,), (1,)), ((), ()))
VMEM_MIB = 51
CHUNKS = ((0, 7), (1, 6), (2, 5), (3, 4))
ORDER = (4, 3, 5, 2, 6, 1, 7)


def fourier_table(n):
    k = np.arange(n)[:, None]
    x = np.arange(n)[None, :]
    h = n // 2
    f = np.where(k <= h, k, k - h)
    angle = (f * x % n) * (2.0 * np.pi / n)
    weight = np.where((k == 0) | (k == h), np.sqrt(1.0 / n), np.sqrt(2.0 / n))
    return (np.where(k <= h, np.cos(angle), np.sin(angle)) * weight).astype(np.float32)


def split(table):
    high = table.astype(jnp.bfloat16)
    low = (table - high.astype(np.float32)).astype(jnp.bfloat16)
    return high, low


def tables(n):
    t = fourier_table(n)
    planes = np.array(CHUNKS)
    k, p, xc, i = np.meshgrid(np.arange(4), np.arange(8), np.arange(8), np.arange(2), indexing="ij")
    x_order = (((p % 4) * 8 + xc) * 16 + (p // 4) * 8 + planes[k, i]).reshape(-1)
    h, zs, j = np.meshgrid(np.arange(2), np.arange(8), np.arange(32), indexing="ij")
    y_order = (zs * 64 + h * 32 + j).reshape(-1)
    bi, g = np.meshgrid(np.arange(16), np.arange(32), indexing="ij")
    b_order = (g * 16 + bi).reshape(-1)
    yh, zs, qj = np.meshgrid(np.arange(2), np.arange(8), np.arange(32), indexing="ij")
    q_order = ((zs * 2 + yh) * 32 + qj).reshape(-1)
    first = split(np.ascontiguousarray(t[:, x_order].T))
    second = split(np.ascontiguousarray(t[b_order][:, y_order].T))
    third = split(np.ascontiguousarray(t[q_order]))
    return np.stack(first + second + third)


def swap_groups(parts, axis, size):
    unit = size // 4
    at = lax.broadcasted_iota(jnp.int32, parts[0].shape, axis)
    low_half = at < 2 * unit
    even = (at // unit) % 2 == 0
    p0, p1, p2, p3 = parts
    a0 = jnp.where(low_half, p0, pltpu.roll(p2, 2 * unit, axis))
    a2 = jnp.where(low_half, pltpu.roll(p0, 2 * unit, axis), p2)
    a1 = jnp.where(low_half, p1, pltpu.roll(p3, 2 * unit, axis))
    a3 = jnp.where(low_half, pltpu.roll(p1, 2 * unit, axis), p3)
    out = []
    for u, v in ((a0, a1), (a2, a3)):
        out.append(jnp.where(even, u, pltpu.roll(v, unit, axis)))
        out.append(jnp.where(even, pltpu.roll(u, 3 * unit, axis), v))
    return out


def kernel(
    x_hbm, t_hbm, e_ref, n_ref,
    x_ref, tab, out1, r1, a, bh, bl, out2, cc, ch, cl, acc, ext, edge, halo, nrm,
    load, store, send, y_sem, x_sem, z_sem, e_sem, h_sem,
):
    row = lax.axis_index("row")
    col = lax.axis_index("col")
    y_lo, xc = row // 8, row % 8
    z, u = col // 2, col % 2
    y = u * 4 + y_lo

    def at_y(d):
        t = (y + d) % 8
        return t, {"row": (t % 4) * 8 + xc, "col": z * 2 + t // 4}

    def at_x(d):
        t = (xc + d) % 8
        return t, {"row": y_lo * 8 + t, "col": col}

    def at_z(d):
        t = (z + d) % 8
        return t, {"row": row, "col": t * 2 + u}

    partner = at_y(4)[1]
    up = {"row": (row + 1) % 32, "col": col}
    down = {"row": (row + 31) % 32, "col": col}
    beside = {"row": row, "col": (col + 15 + 2 * u) % 16}
    beyond = {"row": row, "col": (col + 2 + 12 * u) % 16}

    barrier = pltpu.get_barrier_semaphore()
    for d in ORDER:
        for at in (at_y, at_x, at_z):
            pl.semaphore_signal(barrier, inc=1, device_id=at(d)[1], device_id_type=MESH)
    for who in (up, down, beside):
        pl.semaphore_signal(barrier, inc=1, device_id=who, device_id_type=MESH)

    def wait(ref, sem):
        pltpu.make_async_copy(ref, ref, sem).wait()

    loads = [pltpu.make_async_copy(t_hbm.at[pl.ds(2 * i, 2)], tab.at[pl.ds(2 * i, 2)], load.at[i]) for i in range(3)]
    loads += [pltpu.make_async_copy(x_hbm.at[c], x_ref.at[c], load.at[3 + c]) for c in range(3)]
    for i in (0, 3, 4, 5, 1, 2):
        loads[i].start()

    def remote(src, dst, s, r, who):
        pltpu.make_async_remote_copy(
            src_ref=src, dst_ref=dst, send_sem=s, recv_sem=r, device_id=who, device_id_type=MESH
        ).start()

    def first(c, k):
        rows = slice(k * 128, (k + 1) * 128)
        got = lax.dot_general(tab[0, rows, :], x_ref[c], NT, preferred_element_type=jnp.float32)
        got += lax.dot_general(tab[1, rows, :], x_ref[c], NT, preferred_element_type=jnp.float32)
        parts = [got[:, w * 128 : (w + 1) * 128].reshape(16, 8, 128) for w in range(4)]
        out1[c, k] = jnp.stack(swap_groups(parts, 1, 8), axis=1).reshape(8, 64, 128)

    def send_y(c, k):
        for d in ORDER:
            t, who = at_y(d)
            remote(out1.at[c, k, t], r1.at[c, k, y], send.at[0], y_sem.at[k * 3 + c], who)
        r1[c, k, y] = out1[c, k, y]

    loads[0].wait()
    for k in range(4):
        for c in range(3):
            if k == 0:
                loads[3 + c].wait()
            first(c, k)
            if c == 0 and k == 0:
                pl.semaphore_wait(barrier, 24)
            send_y(c, k)
    loads[1].wait()
    loads[2].wait()

    def send_x(j):
        c, k = j % 3, j // 3
        own = pl.ds(pl.multiple_of(xc * 8, 8), 8)
        wait(r1.at[c, k, pl.ds(0, 7)], y_sem.at[j])
        for d in ORDER:
            t, who = at_x(d)
            remote(
                r1.at[c, k, :, pl.ds(pl.multiple_of(t * 8, 8), 8), :],
                a.at[c, k, :, own, :],
                send.at[1], x_sem.at[j], who,
            )
        a[c, k, :, own, :] = r1[c, k, :, own, :]

    def second(j):
        c, k = j % 3, j // 3
        wait(a.at[c, k, pl.ds(0, 7)], x_sem.at[j])
        for w in range(4):
            for pair in range(2):
                parts = []
                for half in range(2):
                    for i in range(2):
                        rows = pl.ds(w * 2 + i, 8, stride=8)
                        s = half * 4 + pair * 2
                        parts.append(jnp.concatenate([a[c, k, s, rows, :], a[c, k, s + 1, rows, :]], axis=0))
                for n, part in enumerate(swap_groups(parts, 1, 128)):
                    high = part.astype(jnp.bfloat16)
                    rows = slice((w * 4 + n) * 32 + pair * 16, (w * 4 + n) * 32 + (pair + 1) * 16)
                    bh[rows, :] = high
                    bl[rows, :] = (part - high.astype(jnp.float32)).astype(jnp.bfloat16)
        for o in range(2):
            rows = pl.ds(pl.multiple_of((u if o else 1 - u) * 256, 256), 256)
            got = jnp.dot(tab[2, rows, :], bh[...], preferred_element_type=jnp.float32)
            got += jnp.dot(tab[3, rows, :], bh[...], preferred_element_type=jnp.float32)
            got += jnp.dot(tab[2, rows, :], bl[...], preferred_element_type=jnp.float32)
            out2[c, k, o] = got.reshape(8, 32, 128)
            for d in ORDER:
                t, who = at_z(d)
                remote(out2.at[c, k, o, t], cc.at[c, k, o, z], send.at[2], z_sem.at[j * 2 + o], who)
            cc[c, k, o, z] = out2[c, k, o, z]

    base = 1 + u * 8

    def third(j):
        c, k = j % 3, j // 3

        def half(o, carry):
            wait(cc.at[c, k, o, pl.ds(0, 7)], z_sem.at[j * 2 + o])
            for zq in range(2):
                parts = [cc[c, k, o, zq * 4 + i] for i in range(4)]
                for n, part in enumerate(swap_groups(parts, 1, 128)):
                    high = part.astype(jnp.bfloat16)
                    rows = slice((n % 2) * 32, (n % 2 + 1) * 32)
                    into = slice((n // 2 * 2 + zq) * 128, (n // 2 * 2 + zq + 1) * 128)
                    ch[rows, into] = high
                    cl[rows, into] = (part - high.astype(jnp.float32)).astype(jnp.bfloat16)
            got = jnp.dot(ch[...], tab[4], preferred_element_type=jnp.float32)
            got += jnp.dot(cl[...], tab[4], preferred_element_type=jnp.float32)
            got += jnp.dot(ch[...], tab[5], preferred_element_type=jnp.float32)
            level = (0.5 * got * got).reshape(2, 32, 512)
            acc[k, o] = jnp.where(c == 0, level, acc[k, o] + level)

            @pl.when((c == 2) & (o == 0))
            def _():
                remote(acc.at[k, 0, 0], ext.at[base + k], send.at[3], e_sem.at[k], partner)
                remote(acc.at[k, 0, 1], ext.at[base + 7 - k], send.at[3], e_sem.at[k], partner)

            return carry

        lax.fori_loop(0, 2, half, 0)

    def step(j, carry):
        @pl.when(j < 12)
        def _():
            send_x(j)

        @pl.when((j > 0) & (j < 13))
        def _():
            second(j - 1)

        @pl.when(j > 2)
        def _():
            third(j - 3)

        return carry

    lax.fori_loop(0, 15, step, 0)

    def line(o, r):
        planes = [(k, 0) for k in range(4)] + [(k, 1) for k in (3, 2, 1, 0)]
        return jnp.concatenate([acc[k, o, i, r : r + 1, :] for k, i in planes], axis=0)

    top, bottom = line(0, 0), line(0, 31)
    edge[2] = jnp.where(u == 0, bottom, top)
    remote(edge.at[2], halo.at[u, u], send.at[4], h_sem.at[4], beyond)
    halo[1 - u, u] = jnp.where(u == 0, top, bottom)
    top, bottom = line(1, 0), line(1, 31)
    edge[0] = jnp.where(u == 0, bottom, top)
    edge[1] = jnp.where(u == 0, top, bottom)
    remote(edge.at[0], halo.at[u, u], send.at[5], h_sem.at[2], partner)
    remote(edge.at[1], halo.at[1 - u, u], send.at[6], h_sem.at[3], beside)
    for k in range(4):
        for i, at in enumerate(CHUNKS[k]):
            ext[base + at] = acc[k, 1, i]

    place = lax.broadcasted_iota(jnp.int32, (32, 512), 0)

    def plane(i, carry):
        centre = ext[i + 1]
        step_x = 0.5 * (ext[i + 2] - ext[i])
        after = jnp.where(place == 31, halo[1, i // 8, pl.ds(i % 8, 1), :], pltpu.roll(centre, 31, 0))
        before = jnp.where(place == 0, halo[0, i // 8, pl.ds(i % 8, 1), :], pltpu.roll(centre, 1, 0))
        step_y = 0.5 * (after - before)
        step_z = 0.5 * (pltpu.roll(centre, 511, 1) - pltpu.roll(centre, 1, 1))
        square = step_x * step_x + step_y * step_y + step_z * step_z
        scale = -lax.rsqrt(jnp.maximum(square, 1.0))
        nrm[0, i] = (step_x * scale).astype(jnp.bfloat16)
        nrm[1, i] = (step_y * scale).astype(jnp.bfloat16)
        nrm[2, i] = (step_z * scale).astype(jnp.bfloat16)
        return carry

    wait(ext.at[pl.ds(1, 2)], e_sem.at[0])
    remote(ext.at[16], ext.at[0], send.at[7], h_sem.at[0], up)
    remote(ext.at[1], ext.at[17], send.at[8], h_sem.at[1], down)
    mine, theirs = pl.ds(8 * u, 8), pl.ds(8 * (1 - u), 8)
    level_mine = pltpu.make_async_copy(ext.at[pl.ds(base, 8)], e_ref.at[mine], store.at[0])
    level_mine.start()
    wait(halo.at[0, 0], h_sem.at[4])
    lax.fori_loop(1 + 8 * u, 7 + 8 * u, plane, 0)
    wait(halo.at[0, 0], h_sem.at[2])
    wait(halo.at[0, 0], h_sem.at[3])
    wait(ext.at[pl.ds(1, 2)], e_sem.at[1])
    lax.fori_loop(7, 9, plane, 0)
    wait(ext.at[0], h_sem.at[0])
    wait(ext.at[17], h_sem.at[1])
    plane(0, 0)
    plane(15, 0)
    normals_mine = pltpu.make_async_copy(nrm.at[:, mine], n_ref.at[:, mine], store.at[1])
    normals_mine.start()
    wait(ext.at[pl.ds(1, 2)], e_sem.at[2])
    plane(9 - 8 * u, 0)
    plane(14 - 8 * u, 0)
    wait(ext.at[pl.ds(1, 2)], e_sem.at[3])
    level_theirs = pltpu.make_async_copy(ext.at[pl.ds(9 - 8 * u, 8)], e_ref.at[theirs], store.at[2])
    level_theirs.start()
    lax.fori_loop(10 - 8 * u, 14 - 8 * u, plane, 0)
    normals_theirs = pltpu.make_async_copy(nrm.at[:, theirs], n_ref.at[:, theirs], store.at[3])
    normals_theirs.start()

    wait(out1.at[:, :, pl.ds(0, 7)], send.at[0])
    wait(a.at[:, :, pl.ds(0, 7)], send.at[1])
    wait(out2.at[:, :, :, pl.ds(0, 7)], send.at[2])
    wait(acc.at[:, 0], send.at[3])
    wait(edge.at[0], send.at[4])
    wait(edge.at[0], send.at[5])
    wait(edge.at[0], send.at[6])
    wait(ext.at[16], send.at[7])
    wait(ext.at[1], send.at[8])
    for out in (level_mine, normals_mine, level_theirs, normals_theirs):
        out.wait()


def body(coefficients):
    members, span_b, span_q, length = coefficients.shape
    data = coefficients.reshape(members, span_b * span_q, length)
    apart = pl.BlockSpec(memory_space=pl.ANY)
    f32, bf16 = jnp.float32, jnp.bfloat16
    return pl.pallas_call(
        kernel,
        out_shape=(
            jax.ShapeDtypeStruct((16, 32, 512), f32),
            jax.ShapeDtypeStruct((3, 16, 32, 512), bf16),
        ),
        in_specs=[pl.BlockSpec(memory_space=pltpu.HBM)] * 2,
        out_specs=(apart, apart),
        scratch_shapes=[
            pltpu.VMEM((3, 512, 512), bf16),
            pltpu.VMEM((6, 512, 512), bf16),
            pltpu.VMEM((3, 4, 8, 64, 128), f32),
            pltpu.VMEM((3, 4, 8, 64, 128), f32),
            pltpu.VMEM((3, 4, 8, 64, 128), f32),
            pltpu.VMEM((512, 128), bf16),
            pltpu.VMEM((512, 128), bf16),
            pltpu.VMEM((3, 4, 2, 8, 32, 128), f32),
            pltpu.VMEM((3, 4, 2, 8, 32, 128), f32),
            pltpu.VMEM((64, 512), bf16),
            pltpu.VMEM((64, 512), bf16),
            pltpu.VMEM((4, 2, 2, 32, 512), f32),
            pltpu.VMEM((18, 32, 512), f32),
            pltpu.VMEM((3, 8, 512), f32),
            pltpu.VMEM((2, 2, 8, 512), f32),
            pltpu.VMEM((3, 16, 32, 512), bf16),
            pltpu.SemaphoreType.DMA((6,)),
            pltpu.SemaphoreType.DMA((4,)),
            pltpu.SemaphoreType.DMA((9,)),
            pltpu.SemaphoreType.DMA((12,)),
            pltpu.SemaphoreType.DMA((12,)),
            pltpu.SemaphoreType.DMA((24,)),
            pltpu.SemaphoreType.DMA((4,)),
            pltpu.SemaphoreType.DMA((5,)),
        ],
        compiler_params=pltpu.CompilerParams(
            collective_id=0, has_side_effects=True, vmem_limit_bytes=VMEM_MIB * 1024 * 1024
        ),
        name="vorticity_normals",
    )(data, tables(length))


def solution(mesh):
    return jax.shard_map(
        body,
        mesh=mesh,
        in_specs=(P(None, "row", "col", None),),
        out_specs=(P("row", "col", None), P(None, "row", "col", None)),
        check_vma=False,
    )
```

```python
import functools

import jax
import jax.numpy as jnp
import numpy as np
from jax import lax
from jax.experimental import pallas as pl
from jax.experimental.pallas import tpu as pltpu
from jax.sharding import PartitionSpec as P

MESH = pl.DeviceIdType.MESH
NT = (((1,), (1,)), ((), ()))
VMEM_MIB = 51
CHUNKS = ((0, 7), (1, 6), (2, 5), (3, 4))
ORDER = (4, 3, 5, 2, 6, 1, 7)


def fourier_table(n):
    k = np.arange(n)[:, None]
    x = np.arange(n)[None, :]
    h = n // 2
    f = np.where(k <= h, k, k - h)
    angle = (f * x % n) * (2.0 * np.pi / n)
    weight = np.where((k == 0) | (k == h), np.sqrt(1.0 / n), np.sqrt(2.0 / n))
    return (np.where(k <= h, np.cos(angle), np.sin(angle)) * weight).astype(np.float32)


def split(table):
    high = table.astype(jnp.bfloat16)
    low = (table - high.astype(np.float32)).astype(jnp.bfloat16)
    return high, low


def tables(n):
    t = fourier_table(n)
    planes = np.array(CHUNKS)
    k, p, xc, i = np.meshgrid(np.arange(4), np.arange(8), np.arange(8), np.arange(2), indexing="ij")
    x_order = (((p % 4) * 8 + xc) * 16 + (p // 4) * 8 + planes[k, i]).reshape(-1)
    h, zs, j = np.meshgrid(np.arange(2), np.arange(8), np.arange(32), indexing="ij")
    y_order = (zs * 64 + h * 32 + j).reshape(-1)
    bi, g = np.meshgrid(np.arange(16), np.arange(32), indexing="ij")
    b_order = (g * 16 + bi).reshape(-1)
    yh, zs, qj = np.meshgrid(np.arange(2), np.arange(8), np.arange(32), indexing="ij")
    q_order = ((zs * 2 + yh) * 32 + qj).reshape(-1)
    first = split(np.ascontiguousarray(t[:, x_order].T))
    second = split(np.ascontiguousarray(t[b_order][:, y_order].T))
    third = split(np.ascontiguousarray(t[q_order]))
    return np.stack(first + second + third)


def swap_groups(parts, axis, size):
    unit = size // 4
    at = lax.broadcasted_iota(jnp.int32, parts[0].shape, axis)
    low_half = at < 2 * unit
    even = (at // unit) % 2 == 0
    p0, p1, p2, p3 = parts
    a0 = jnp.where(low_half, p0, pltpu.roll(p2, 2 * unit, axis))
    a2 = jnp.where(low_half, pltpu.roll(p0, 2 * unit, axis), p2)
    a1 = jnp.where(low_half, p1, pltpu.roll(p3, 2 * unit, axis))
    a3 = jnp.where(low_half, pltpu.roll(p1, 2 * unit, axis), p3)
    out = []
    for u, v in ((a0, a1), (a2, a3)):
        out.append(jnp.where(even, u, pltpu.roll(v, unit, axis)))
        out.append(jnp.where(even, pltpu.roll(u, 3 * unit, axis), v))
    return out


def kernel(
    x_hbm, t_hbm, e_ref, n_ref,
    x_ref, tab, out1, r1, a, bh, bl, out2, cc, ch, cl, acc, ext, edge, halo, nrm,
    load, store, send, y_sem, x_sem, z_sem, e_sem, h_sem,
):
    row = lax.axis_index("row")
    col = lax.axis_index("col")
    y_lo, xc = row // 8, row % 8
    z, u = col // 2, col % 2
    y = u * 4 + y_lo

    def at_y(d):
        t = (y + d) % 8
        return t, {"row": (t % 4) * 8 + xc, "col": z * 2 + t // 4}

    def at_x(d):
        t = (xc + d) % 8
        return t, {"row": y_lo * 8 + t, "col": col}

    def at_z(d):
        t = (z + d) % 8
        return t, {"row": row, "col": t * 2 + u}

    partner = at_y(4)[1]
    up = {"row": (row + 1) % 32, "col": col}
    down = {"row": (row + 31) % 32, "col": col}
    beside = {"row": row, "col": (col + 15 + 2 * u) % 16}
    beyond = {"row": row, "col": (col + 2 + 12 * u) % 16}

    barrier = pltpu.get_barrier_semaphore()
    for d in ORDER:
        for at in (at_y, at_x, at_z):
            pl.semaphore_signal(barrier, inc=1, device_id=at(d)[1], device_id_type=MESH)
    for who in (up, down, beside):
        pl.semaphore_signal(barrier, inc=1, device_id=who, device_id_type=MESH)

    def wait(ref, sem):
        pltpu.make_async_copy(ref, ref, sem).wait()

    loads = [pltpu.make_async_copy(t_hbm.at[pl.ds(2 * i, 2)], tab.at[pl.ds(2 * i, 2)], load.at[i]) for i in range(3)]
    loads += [pltpu.make_async_copy(x_hbm.at[c], x_ref.at[c], load.at[3 + c]) for c in range(3)]
    for i in (0, 3, 4, 5, 1, 2):
        loads[i].start()

    def remote(src, dst, s, r, who):
        pltpu.make_async_remote_copy(
            src_ref=src, dst_ref=dst, send_sem=s, recv_sem=r, device_id=who, device_id_type=MESH
        ).start()

    def first(c, k):
        rows = slice(k * 128, (k + 1) * 128)
        got = lax.dot_general(tab[0, rows, :], x_ref[c], NT, preferred_element_type=jnp.float32)
        got += lax.dot_general(tab[1, rows, :], x_ref[c], NT, preferred_element_type=jnp.float32)
        parts = [got[:, w * 128 : (w + 1) * 128].reshape(16, 8, 128) for w in range(4)]
        out1[c, k] = jnp.stack(swap_groups(parts, 1, 8), axis=1).reshape(8, 64, 128)

    def send_y(c, k):
        for d in ORDER:
            t, who = at_y(d)
            remote(out1.at[c, k, t], r1.at[c, k, y], send.at[0], y_sem.at[k * 3 + c], who)
        r1[c, k, y] = out1[c, k, y]

    loads[0].wait()
    for k in range(4):
        for c in range(3):
            if k == 0:
                loads[3 + c].wait()
            first(c, k)
            if c == 0 and k == 0:
                pl.semaphore_wait(barrier, 24)
            send_y(c, k)
    loads[1].wait()
    loads[2].wait()

    def send_x(j):
        c, k = j % 3, j // 3
        own = pl.ds(pl.multiple_of(xc * 8, 8), 8)
        wait(r1.at[c, k, pl.ds(0, 7)], y_sem.at[j])
        for d in ORDER:
            t, who = at_x(d)
            remote(
                r1.at[c, k, :, pl.ds(pl.multiple_of(t * 8, 8), 8), :],
                a.at[c, k, :, own, :],
                send.at[1], x_sem.at[j], who,
            )
        a[c, k, :, own, :] = r1[c, k, :, own, :]

    def second(j):
        c, k = j % 3, j // 3
        wait(a.at[c, k, pl.ds(0, 7)], x_sem.at[j])
        for w in range(4):
            for pair in range(2):
                parts = []
                for half in range(2):
                    for i in range(2):
                        rows = pl.ds(w * 2 + i, 8, stride=8)
                        s = half * 4 + pair * 2
                        parts.append(jnp.concatenate([a[c, k, s, rows, :], a[c, k, s + 1, rows, :]], axis=0))
                for n, part in enumerate(swap_groups(parts, 1, 128)):
                    high = part.astype(jnp.bfloat16)
                    rows = slice((w * 4 + n) * 32 + pair * 16, (w * 4 + n) * 32 + (pair + 1) * 16)
                    bh[rows, :] = high
                    bl[rows, :] = (part - high.astype(jnp.float32)).astype(jnp.bfloat16)
        for o in range(2):
            rows = pl.ds(pl.multiple_of((u if o else 1 - u) * 256, 256), 256)
            got = jnp.dot(tab[2, rows, :], bh[...], preferred_element_type=jnp.float32)
            got += jnp.dot(tab[3, rows, :], bh[...], preferred_element_type=jnp.float32)
            got += jnp.dot(tab[2, rows, :], bl[...], preferred_element_type=jnp.float32)
            out2[c, k, o] = got.reshape(8, 32, 128)
            for d in ORDER:
                t, who = at_z(d)
                remote(out2.at[c, k, o, t], cc.at[c, k, o, z], send.at[2], z_sem.at[j * 2 + o], who)
            cc[c, k, o, z] = out2[c, k, o, z]

    base = 1 + u * 8

    def third(j):
        c, k = j % 3, j // 3

        def half(o, carry):
            wait(cc.at[c, k, o, pl.ds(0, 7)], z_sem.at[j * 2 + o])
            for zq in range(2):
                parts = [cc[c, k, o, zq * 4 + i] for i in range(4)]
                for n, part in enumerate(swap_groups(parts, 1, 128)):
                    high = part.astype(jnp.bfloat16)
                    rows = slice((n % 2) * 32, (n % 2 + 1) * 32)
                    into = slice((n // 2 * 2 + zq) * 128, (n // 2 * 2 + zq + 1) * 128)
                    ch[rows, into] = high
                    cl[rows, into] = (part - high.astype(jnp.float32)).astype(jnp.bfloat16)
            got = jnp.dot(ch[...], tab[4], preferred_element_type=jnp.float32)
            got += jnp.dot(cl[...], tab[4], preferred_element_type=jnp.float32)
            got += jnp.dot(ch[...], tab[5], preferred_element_type=jnp.float32)
            level = (0.5 * got * got).reshape(2, 32, 512)
            acc[k, o] = jnp.where(c == 0, level, acc[k, o] + level)

            @pl.when((c == 2) & (o == 0))
            def _():
                remote(acc.at[k, 0, 0], ext.at[base + k], send.at[3], e_sem.at[k], partner)
                remote(acc.at[k, 0, 1], ext.at[base + 7 - k], send.at[3], e_sem.at[k], partner)

            return carry

        lax.fori_loop(0, 2, half, 0)

    def step(j, carry):
        @pl.when(j < 12)
        def _():
            send_x(j)

        @pl.when((j > 0) & (j < 13))
        def _():
            second(j - 1)

        @pl.when(j > 2)
        def _():
            third(j - 3)

        return carry

    lax.fori_loop(0, 15, step, 0)

    def line(o, r):
        planes = [(k, 0) for k in range(4)] + [(k, 1) for k in (3, 2, 1, 0)]
        return jnp.concatenate([acc[k, o, i, r : r + 1, :] for k, i in planes], axis=0)

    top, bottom = line(0, 0), line(0, 31)
    edge[2] = jnp.where(u == 0, bottom, top)
    remote(edge.at[2], halo.at[u, u], send.at[4], h_sem.at[4], beyond)
    halo[1 - u, u] = jnp.where(u == 0, top, bottom)
    top, bottom = line(1, 0), line(1, 31)
    edge[0] = jnp.where(u == 0, bottom, top)
    edge[1] = jnp.where(u == 0, top, bottom)
    remote(edge.at[0], halo.at[u, u], send.at[5], h_sem.at[2], partner)
    remote(edge.at[1], halo.at[1 - u, u], send.at[6], h_sem.at[3], beside)
    for k in range(4):
        for i, at in enumerate(CHUNKS[k]):
            ext[base + at] = acc[k, 1, i]

    place = lax.broadcasted_iota(jnp.int32, (32, 512), 0)

    def plane(i, carry):
        centre = ext[i + 1]
        step_x = 0.5 * (ext[i + 2] - ext[i])
        after = jnp.where(place == 31, halo[1, i // 8, pl.ds(i % 8, 1), :], pltpu.roll(centre, 31, 0))
        before = jnp.where(place == 0, halo[0, i // 8, pl.ds(i % 8, 1), :], pltpu.roll(centre, 1, 0))
        step_y = 0.5 * (after - before)
        step_z = 0.5 * (pltpu.roll(centre, 511, 1) - pltpu.roll(centre, 1, 1))
        square = step_x * step_x + step_y * step_y + step_z * step_z
        scale = -lax.rsqrt(jnp.maximum(square, 1.0))
        nrm[0, i] = (step_x * scale).astype(jnp.bfloat16)
        nrm[1, i] = (step_y * scale).astype(jnp.bfloat16)
        nrm[2, i] = (step_z * scale).astype(jnp.bfloat16)
        return carry

    wait(ext.at[pl.ds(1, 2)], e_sem.at[0])
    remote(ext.at[16], ext.at[0], send.at[7], h_sem.at[0], up)
    remote(ext.at[1], ext.at[17], send.at[8], h_sem.at[1], down)
    mine, theirs = pl.ds(8 * u, 8), pl.ds(8 * (1 - u), 8)
    level_mine = pltpu.make_async_copy(ext.at[pl.ds(base, 8)], e_ref.at[mine], store.at[0])
    level_mine.start()
    wait(halo.at[0, 0], h_sem.at[4])
    lax.fori_loop(1 + 8 * u, 7 + 8 * u, plane, 0)
    wait(halo.at[0, 0], h_sem.at[2])
    wait(halo.at[0, 0], h_sem.at[3])
    wait(ext.at[pl.ds(1, 2)], e_sem.at[1])
    lax.fori_loop(7, 9, plane, 0)
    wait(ext.at[0], h_sem.at[0])
    wait(ext.at[17], h_sem.at[1])
    plane(0, 0)
    plane(15, 0)
    normals_mine = pltpu.make_async_copy(nrm.at[:, mine], n_ref.at[:, mine], store.at[1])
    normals_mine.start()
    wait(ext.at[pl.ds(1, 2)], e_sem.at[2])
    plane(9 - 8 * u, 0)
    plane(14 - 8 * u, 0)
    wait(ext.at[pl.ds(1, 2)], e_sem.at[3])
    level_theirs = pltpu.make_async_copy(ext.at[pl.ds(9 - 8 * u, 8)], e_ref.at[theirs], store.at[2])
    level_theirs.start()
    lax.fori_loop(10 - 8 * u, 14 - 8 * u, plane, 0)
    normals_theirs = pltpu.make_async_copy(nrm.at[:, theirs], n_ref.at[:, theirs], store.at[3])
    normals_theirs.start()

    wait(out1.at[:, :, pl.ds(0, 7)], send.at[0])
    wait(a.at[:, :, pl.ds(0, 7)], send.at[1])
    wait(out2.at[:, :, :, pl.ds(0, 7)], send.at[2])
    wait(acc.at[:, 0], send.at[3])
    wait(edge.at[0], send.at[4])
    wait(edge.at[0], send.at[5])
    wait(edge.at[0], send.at[6])
    wait(ext.at[16], send.at[7])
    wait(ext.at[1], send.at[8])
    for out in (level_mine, normals_mine, level_theirs, normals_theirs):
        out.wait()


def write_out(level_in, normals_in, level_out, normals_out, sem):
    pairs = ((level_in, level_out), (normals_in, normals_out))
    copies = [pltpu.make_async_copy(a, b, sem.at[i]) for i, (a, b) in enumerate(pairs)]
    for copy in copies:
        copy.start()
    for copy in copies:
        copy.wait()


def body(coefficients):
    members, span_b, span_q, length = coefficients.shape
    data = coefficients.reshape(members, span_b * span_q, length)
    apart = pl.BlockSpec(memory_space=pl.ANY)
    f32, bf16 = jnp.float32, jnp.bfloat16
    shapes = (
        jax.ShapeDtypeStruct((16, 32, 512), f32),
        jax.ShapeDtypeStruct((3, 16, 32, 512), bf16),
    )
    results = pl.pallas_call(
        kernel,
        out_shape=shapes,
        in_specs=[pl.BlockSpec(memory_space=pltpu.HBM)] * 2,
        out_specs=(apart, apart),
        scratch_shapes=[
            pltpu.VMEM((3, 512, 512), bf16),
            pltpu.VMEM((6, 512, 512), bf16),
            pltpu.VMEM((3, 4, 8, 64, 128), f32),
            pltpu.VMEM((3, 4, 8, 64, 128), f32),
            pltpu.VMEM((3, 4, 8, 64, 128), f32),
            pltpu.VMEM((512, 128), bf16),
            pltpu.VMEM((512, 128), bf16),
            pltpu.VMEM((3, 4, 2, 8, 32, 128), f32),
            pltpu.VMEM((3, 4, 2, 8, 32, 128), f32),
            pltpu.VMEM((64, 512), bf16),
            pltpu.VMEM((64, 512), bf16),
            pltpu.VMEM((4, 2, 2, 32, 512), f32),
            pltpu.VMEM((18, 32, 512), f32),
            pltpu.VMEM((3, 8, 512), f32),
            pltpu.VMEM((2, 2, 8, 512), f32),
            pltpu.VMEM((3, 16, 32, 512), bf16),
            pltpu.SemaphoreType.DMA((6,)),
            pltpu.SemaphoreType.DMA((4,)),
            pltpu.SemaphoreType.DMA((9,)),
            pltpu.SemaphoreType.DMA((12,)),
            pltpu.SemaphoreType.DMA((12,)),
            pltpu.SemaphoreType.DMA((24,)),
            pltpu.SemaphoreType.DMA((4,)),
            pltpu.SemaphoreType.DMA((5,)),
        ],
        compiler_params=pltpu.CompilerParams(
            collective_id=0, has_side_effects=True, vmem_limit_bytes=VMEM_MIB * 1024 * 1024
        ),
        name="vorticity_normals",
    )(data, tables(length))
    return pl.pallas_call(
        write_out,
        out_shape=shapes,
        in_specs=[pl.BlockSpec(memory_space=pltpu.VMEM)] * 2,
        out_specs=(apart, apart),
        scratch_shapes=[pltpu.SemaphoreType.DMA((2,))],
        compiler_params=pltpu.CompilerParams(vmem_limit_bytes=8 * 1024 * 1024),
        name="write_out",
    )(*results)


def solution(mesh):
    return jax.shard_map(
        body,
        mesh=mesh,
        in_specs=(P(None, "row", "col", None),),
        out_specs=(P("row", "col", None), P(None, "row", "col", None)),
        check_vma=False,
    )
```
